1024 devices in a mesh: dp: 128 (over y_lo, z, core), tensor: 4 (over x), group: 2 (over y_hi).
Axes of the slice: x: 4, y: 4 (y_hi: 2, y_lo: 2; y = y_hi * 2 + y_lo), z: 32, core: 2. Of those that a mesh axis runs over, the one named last changes fastest.
Arguments:
- tokens: bfloat16 [32768, 5120], P(('dp', 'group')), may hold values from -6 to 6
- cotangent: bfloat16 [32768, 1024], P(('dp', 'group'), 'tensor'), may hold values from -0.032958984 to 0.032958984
- counts: int32 [256], replicated, may hold values from 32 to 128, as said below
- old_offsets: int32 [8, 129], replicated, may hold values from 0 to 655360, as said below
- old_master: float32 [8, 128, 6400], P(('tensor', 'group'), 'dp'), may hold values from -0.078125 to 0.078125
- old_moment: float32 [8, 128, 6400], P(('tensor', 'group'), 'dp'), may hold values from -3 to 3
- old_variance: float32 [8, 128, 6400], P(('tensor', 'group'), 'dp'), may hold values from 0.001 to 1
- old_grad: float32 [8, 128, 6400], P(('tensor', 'group'), 'dp'), may hold values from -6 to 6
Outputs:
- activated: bfloat16 [32768, 1024], P(('dp', 'group'), 'tensor')
- new_master: float32 [5120, 1024], P(('dp', 'group'), 'tensor')
- new_moment: float32 [5120, 1024], P(('dp', 'group'), 'tensor')
- new_variance: float32 [5120, 1024], P(('dp', 'group'), 'tensor')
The draws below stay inside these ranges and needn't reach their ends.
Inputs may be any that keep to these rules, and one draw needn't show every extreme that they name: `counts`: each new data rank has between 32 and 128 live tokens, which fill its first slots; in every draw some rank has exactly 128. `old_offsets`: each row starts at 0 and ends at 655360; entry p lies within 640 of p * 5120; in every row some entry p with 0 < p < 128 equals p * 5120 + 640.
All inputs are finite; a program needn't handle non-finite values.
Results may differ from the reference program's by a relative error of at most 0.0051.
Values may be sent and summed in bfloat16 or wider, within the bound.
A program may use at most 32 MiB of HBM per device.

```python
import math
import jax
import jax.numpy as jnp

D = 5120
KV = 1024
TOK = 128
DATA = 256
TOKENS = 32768
OLD_RANKS = 128
OLD_SLABS = 8
OLD_COLS = 128
SHARD = 5120
SLACK = 640
WINDOW = 6400


def draw_counts(key, part):
    drawn = jax.random.randint(jax.random.fold_in(key, 11), (DATA,), TOK // 4, TOK + 1)
    chosen = jax.random.randint(jax.random.fold_in(key, 12), (), 0, DATA)
    return jnp.where(jnp.arange(DATA) == chosen, TOK, drawn).astype(jnp.int32)


def draw_old_offsets(key, part):
    offset_shift = jax.random.randint(jax.random.fold_in(key, 21), (OLD_SLABS, OLD_RANKS + 1), -SLACK, SLACK + 1)
    chosen = jax.random.randint(jax.random.fold_in(key, 22), (OLD_SLABS, 1), 1, OLD_RANKS)
    column_index = jnp.arange(OLD_RANKS + 1)[None, :]
    offset_shift = jnp.where(column_index == chosen, SLACK, offset_shift)
    offset_shift = jnp.where((column_index == 0) | (column_index == OLD_RANKS), 0, offset_shift)
    return (column_index * SHARD + offset_shift).astype(jnp.int32)


def shard_levels(key, extent, cuts, least, top_value):
    def one(axis_at, shards_of):
        draws = jax.random.uniform(jax.random.fold_in(jax.random.fold_in(key, 6), axis_at), (shards_of,), jnp.float32, least / len(cuts), top_value / len(cuts))
        return jnp.repeat(jnp.exp(draws), extent[axis_at] // shards_of).reshape((-1,) + (1,) * (len(extent) - axis_at - 1))

    factor_of = one(*cuts[0])
    for cut in cuts[1:]:
        factor_of = factor_of * one(*cut)
    return factor_of


def noise(own_key, shape, deviation, most, shards=(), kind=jnp.bfloat16):
    values = jax.random.normal(own_key, shape, jnp.float32) * deviation
    if len(shards) > 0:
        values = shard_levels(own_key, shape, shards, -0.22, 0.18) * values
    return jnp.clip(values, min=-most, max=most).astype(kind)


def setup_inputs(seed: int = 0) -> dict:
    streams_of = jax.random.split(jax.random.key(seed), 9)
    tokens = noise(streams_of[0], (TOKENS, D), 1.0, 6.0, ((0, 256),))
    cotangent = noise(streams_of[1], (TOKENS, KV), (TOKENS ** -0.5), 0.032958984, ((0, 256), (1, 4)))
    counts = draw_counts(jax.random.fold_in(streams_of[8], 71), 0)
    old_offsets = draw_old_offsets(jax.random.fold_in(streams_of[8], 71), 0)
    old_master = noise(streams_of[4], (OLD_SLABS, OLD_RANKS, WINDOW), D ** -0.5, 0.078125, ((0, 8), (1, 128)), jnp.float32)
    old_moment = noise(streams_of[5], (OLD_SLABS, OLD_RANKS, WINDOW), 0.5, 3.0, ((0, 8), (1, 128)), jnp.float32)
    old_variance = jnp.clip(jnp.exp(math.log(1.0) - 6.9077552 * jax.random.uniform(streams_of[6], (OLD_SLABS, OLD_RANKS, WINDOW), jnp.float32) ** shard_levels(streams_of[6], (OLD_SLABS, OLD_RANKS, WINDOW), ((0, 8), (1, 128)), -0.2, 0.2)), 0.001, 1.0)
    old_grad = noise(streams_of[7], (OLD_SLABS, OLD_RANKS, WINDOW), 1.0, 6.0, ((0, 8), (1, 128)), jnp.float32)
    return {"tokens": tokens, "cotangent": cotangent, "counts": counts, "old_offsets": old_offsets, "old_master": old_master, "old_moment": old_moment, "old_variance": old_variance, "old_grad": old_grad}


beta_one = 0.9
beta_two = 0.95
epsilon = 1e-08
learn_rate = 0.001
weight_decay = 0.1
first_step = 3.0
second_step = 4.0

def adam_update(master, moment, variance, gradient, step_count):
    moment = beta_one * moment + (1.0 - beta_one) * gradient
    variance = beta_two * variance + (1.0 - beta_two) * gradient * gradient
    fix_one = 1.0 - beta_one ** step_count
    fix_two = 1.0 - beta_two ** step_count
    update = moment / fix_one / (jnp.sqrt(variance / fix_two) + epsilon) + weight_decay * master
    return (master - learn_rate * update, moment, variance)

def rebuild(windows, old_offsets):
    slab_count, old_ranks, window = windows.shape[1:]
    position = jnp.arange(old_ranks, dtype=jnp.int32)[:, None] * SHARD - SLACK + jnp.arange(window, dtype=jnp.int32)[None, :]
    low_edge = old_offsets[:, :-1][:, :, None]
    high_edge = old_offsets[:, 1:][:, :, None]
    is_live = (position[None] >= low_edge) & (position[None] < high_edge)
    masked = jnp.where(is_live[None], windows, jnp.float32(0.0))
    target = jnp.clip(position, 0, SHARD * old_ranks - 1).astype(jnp.int32)
    flat_state = jnp.zeros((3, slab_count, SHARD * old_ranks), jnp.float32)
    flat_state = flat_state.at[:, :, target].add(masked)
    whole_state = flat_state.reshape(3, slab_count, D, OLD_COLS).transpose(0, 2, 1, 3)
    return whole_state.reshape(3, D, KV)

def reference(tokens, cotangent, counts, old_offsets, old_master, old_moment, old_variance, old_grad):
    master, moment, variance = adam_update(old_master, old_moment, old_variance, old_grad, first_step)
    states = rebuild(jnp.stack([master, moment, variance]), old_offsets)
    weights = states[0].astype(jnp.bfloat16)
    preact = jnp.dot(tokens, weights, preferred_element_type=jnp.float32)
    activated = jax.nn.silu(preact).astype(jnp.bfloat16)
    sigmoid_z = jax.nn.sigmoid(preact)
    derivative = sigmoid_z * (1.0 + preact * (1.0 - sigmoid_z))
    row_ids = jnp.arange(TOKENS, dtype=jnp.int32)
    is_live = row_ids % TOK < counts[row_ids // TOK]
    delta = jnp.where(is_live[:, None], cotangent.astype(jnp.float32) * derivative, jnp.float32(0.0)).astype(jnp.bfloat16)
    gradient = jnp.dot(tokens.T, delta, preferred_element_type=jnp.float32)
    new_master, new_moment, new_variance = adam_update(states[0], states[1], states[2], gradient, second_step)
    return (activated, new_master, new_moment, new_variance)
```

```python
import functools

import jax
import jax.numpy as jnp
from jax import lax
from jax.experimental import pallas as pl
from jax.experimental.pallas import tpu as pltpu
from jax.sharding import PartitionSpec as P

MESH = pl.DeviceIdType.MESH
F32 = jnp.float32
BF16 = jnp.bfloat16

beta_one = 0.9
beta_two = 0.95
epsilon = 1e-08
learn_rate = 0.001
weight_decay = 0.1
first_step = 3.0
second_step = 4.0

LANES = 128
STRIDE = 4


def adam_update(master, moment, variance, gradient, step_count):
    moment = beta_one * moment + (1.0 - beta_one) * gradient
    variance = beta_two * variance + (1.0 - beta_two) * gradient * gradient
    fix_one = 1.0 - beta_one**step_count
    fix_two = 1.0 - beta_two**step_count
    update = moment / fix_one / (jnp.sqrt(variance / fix_two) + epsilon) + weight_decay * master
    return (master - learn_rate * update, moment, variance)


def kernel(
    dp_size,
    offsets,
    counts,
    tok_hbm,
    cot,
    old_master,
    old_moment,
    old_variance,
    old_grad,
    act_out,
    master_out,
    moment_out,
    variance_out,
    tok,
    tok_t,
    old,
    live_state,
    edge_out,
    edge_in,
    state,
    w,
    w_flat,
    parts,
    core_in,
    y_in,
    z_sum,
    near_in,
    plus_out,
    plus_in,
    minus_out,
    minus_in,
    tile_out,
    tile_in,
    tok_sem,
    edge_sems,
    ring_send,
    z_recv,
    near_send,
    y_send,
    y_recv,
    core_send,
    core_recv,
    part_send,
    part_recv,
    sum_send,
    sum_recv,
    window_send,
    window_recv,
    plus_sems,
    minus_sems,
    tile_sems,
):
    depth = dp_size // 4
    members = depth // STRIDE
    half = members // 2
    rows = state.shape[1]
    window_rows = old.shape[1]
    margin = (window_rows - rows) // 2
    tile = rows // 2

    dp = lax.axis_index("dp")
    group = lax.axis_index("group")
    tensor = lax.axis_index("tensor")
    core = lax.rem(dp, 2)
    z = lax.rem(lax.div(dp, 2), depth)
    y_lo = lax.div(dp, 2 * depth)
    a = lax.div(z, STRIDE)
    b = lax.rem(z, STRIDE)

    def device(dz=0, flip_lo=0, flip_group=0, flip_core=0):
        to_z = lax.rem(z + dz + depth, depth)
        to_lo = 1 - y_lo if flip_lo else y_lo
        to_core = 1 - core if flip_core else core
        to_group = 1 - group if flip_group else group
        return {"dp": (to_lo * depth + to_z) * 2 + to_core, "group": to_group}

    right = {"dp": lax.rem(dp + 1, dp_size), "group": group}
    left = {"dp": lax.rem(dp + dp_size - 1, dp_size), "group": group}
    other_core = device(flip_core=1)
    y_flips = ((1, 0), (1, 1), (0, 1))
    y_peers = [device(flip_lo=l, flip_group=g) for l, g in y_flips]

    def remote(src, dst, send_sem, recv_sem, to):
        return pltpu.make_async_remote_copy(
            src_ref=src,
            dst_ref=dst,
            send_sem=send_sem,
            recv_sem=recv_sem,
            device_id=to,
            device_id_type=MESH,
        )

    pending = []

    def send(src, dst, send_sem, recv_sem, to):
        copy = remote(src, dst, send_sem, recv_sem, to)
        copy.start()
        pending.append(copy)

    def arrived(dst, recv_sem):
        remote(dst, dst, recv_sem, recv_sem, other_core).wait_recv()

    tok_copy = pltpu.make_async_copy(tok_hbm, tok, tok_sem)
    tok_copy.start()

    barrier = pltpu.get_barrier_semaphore()
    greeted = [right, left, other_core, *y_peers]
    greeted += [device(dz=d) for d in (STRIDE, -STRIDE, 1, -1, 2, -2)]
    for peer in greeted:
        pl.semaphore_signal(barrier, inc=1, device_id=peer, device_id_type=MESH)

    for r in range(window_rows):
        lanes = slice(r * LANES, (r + 1) * LANES)
        for i, ref in enumerate((old_master, old_moment, old_variance, old_grad)):
            old[i, r : r + 1, :] = ref[0, :, lanes]
    updated = adam_update(old[0], old[1], old[2], old[3], first_step)
    shape = (window_rows, LANES)
    position = (
        dp * (rows * LANES)
        - margin * LANES
        + lax.broadcasted_iota(jnp.int32, shape, 0) * LANES
        + lax.broadcasted_iota(jnp.int32, shape, 1)
    )
    slab = tensor * 2 + group
    low, high = offsets[slab, dp], offsets[slab, dp + 1]
    is_live = (position >= low) & (position < high)
    for i in range(3):
        live_state[i] = jnp.where(is_live, updated[i], F32(0.0))
    for i in range(3):
        edge_out[0, i] = live_state[i, rows + margin : window_rows, :]
        edge_out[1, i] = live_state[i, 0:margin, :]
    pl.semaphore_wait(barrier, len(greeted))
    send(edge_out.at[0], edge_in.at[0], edge_sems.at[0], edge_sems.at[2], right)
    send(edge_out.at[1], edge_in.at[1], edge_sems.at[1], edge_sems.at[3], left)
    for i in range(3):
        state[i] = live_state[i, margin : margin + rows, :]
    arrived(edge_in.at[0], edge_sems.at[2])
    arrived(edge_in.at[1], edge_sems.at[3])
    for i in range(3):
        state[i, 0:margin, :] += edge_in[0, i]
        state[i, rows - margin : rows, :] += edge_in[1, i]

    line = w.at[group, y_lo, core]
    line[z] = state[0].astype(BF16)

    def at(k):
        return lax.rem(z + STRIDE * k + depth, depth)

    def ring(slot, step, direction):
        index = step if direction > 0 else half + step
        send(line.at[slot], line.at[slot], ring_send.at[index], z_recv.at[slot], device(dz=direction * STRIDE))

    def near(slot):
        block = lax.div(slot, STRIDE)
        far = 2 - 4 * lax.rem(block, 2)
        for i, d in enumerate((1, -1, far)):
            send(line.at[slot], line.at[slot], near_send.at[i, block], z_recv.at[slot], device(dz=d))

    def along_y(k):
        block = lax.rem(a + k + members, members)
        for d in range(1, STRIDE):
            slot = block * STRIDE + lax.rem(b + d, STRIDE)
            arrived(line.at[slot], z_recv.at[slot])
        piece = line.at[pl.ds(block * STRIDE, STRIDE)]
        for i, peer in enumerate(y_peers):
            send(piece, piece, y_send.at[i, block], y_recv.at[i, block], peer)

    ring(z, 0, 1)
    if half > 1:
        ring(z, 0, -1)
    near(z)

    tok_copy.wait()
    for i in range(tok.shape[1] // LANES):
        lanes = slice(i * LANES, (i + 1) * LANES)
        tok_t[lanes, :] = tok[:, lanes].T

    for k in range(1, half + 1):
        slot = at(-k)
        arrived(line.at[slot], z_recv.at[slot])
        if k < half:
            ring(slot, k, 1)
        near(slot)
        if k < half:
            slot = at(k)
            arrived(line.at[slot], z_recv.at[slot])
            if k < half - 1:
                ring(slot, k, -1)
            near(slot)
        along_y(1 - k)
        if k > 1:
            along_y(k - 1)
    along_y(half)

    def to_core(i, lo, g):
        src = w.at[g, lo, core]
        send(src, src, core_send.at[i], core_recv.at[i], other_core)

    def lines(i):
        l, g = ((0, 0),) [0] if i == 0 else y_flips[i - 1]
        return (1 - y_lo if l else y_lo), (1 - group if g else group)

    to_core(0, y_lo, group)
    for i in range(3):
        lo, g = lines(i + 1)
        for block in range(members):
            src = w.at[g, lo, core, pl.ds(block * STRIDE, STRIDE)]
            arrived(src, y_recv.at[i, block])
        to_core(i + 1, lo, g)
    for i in range(4):
        lo, g = lines(i)
        arrived(w.at[g, lo, 1 - core], core_recv.at[i])

    def flatten(zz, carry):
        for lo in range(2):
            start = pl.multiple_of((lo * depth + zz) * (2 * rows), 2 * rows)
            for g in range(2):
                both = jnp.concatenate([w[g, lo, 0, zz], w[g, lo, 1, zz]], axis=0)
                w_flat[pl.ds(start, 2 * rows), g * LANES : (g + 1) * LANES] = both
        return carry

    lax.fori_loop(0, depth, flatten, 0)
    preact = jnp.dot(tok[...], w_flat[...], preferred_element_type=F32)
    sigmoid_z = jax.nn.sigmoid(preact)
    act_out[...] = (preact * sigmoid_z).astype(BF16)
    derivative = sigmoid_z * (1.0 + preact * (1.0 - sigmoid_z))
    my_count = counts[dp * 2 + group]
    row_live = lax.broadcasted_iota(jnp.int32, preact.shape, 0) < my_count
    delta = jnp.where(row_live, cot[...].astype(F32) * derivative, F32(0.0)).astype(BF16)

    order = [half] + [s * k for k in range(half - 1, 0, -1) for s in (1, -1)] + [0]
    blocks = [lax.rem(a + k + members, members) for k in order]
    for block in blocks:
        for lo in range(2):
            count = STRIDE * 2 * rows
            start = pl.multiple_of((lo * depth + block * STRIDE) * (2 * rows), count)
            part = jnp.dot(tok_t[pl.ds(start, count), :], delta, preferred_element_type=F32)
            for zz in range(STRIDE):
                for c in range(2):
                    top = (zz * 2 + c) * rows
                    for g in range(2):
                        parts[c, block, g, lo, zz] = part[top : top + rows, g * LANES : (g + 1) * LANES].astype(BF16)
        send(parts.at[1 - core, block], core_in.at[block], part_send.at[block], part_recv.at[block], other_core)
    for block in blocks:
        arrived(core_in.at[block], part_recv.at[block])
        both = parts[core, block].astype(F32) + core_in[block].astype(F32)
        parts[core, block] = both.astype(BF16)
        for i, (l, g) in enumerate(y_flips):
            lo = 1 - y_lo if l else y_lo
            gg = 1 - group if g else group
            send(parts.at[core, block, gg, lo], y_in.at[i, block], sum_send.at[i, block], sum_recv.at[i, block], y_peers[i])

    def over_y(j):
        block = blocks[j]
        total = parts[core, block, group, y_lo].astype(F32)
        for i in range(3):
            arrived(y_in.at[i, block], sum_recv.at[i, block])
            total += y_in[i, block].astype(F32)
        z_sum[block] = total.astype(BF16)
        far = 2 - 4 * lax.rem(block, 2)
        for i, (d, dz) in enumerate(((1, 1), (3, -1), (2, far))):
            src = z_sum.at[block, lax.rem(b + d, STRIDE)]
            send(src, near_in.at[i, block], window_send.at[i, block], window_recv.at[i, block], device(dz=dz))

    def over_ring(j):
        block, k = blocks[j], order[j]
        total = z_sum[block, b].astype(F32)
        for i in range(3):
            arrived(near_in.at[i, block], window_recv.at[i, block])
            total += near_in[i, block].astype(F32)
        if k >= 0 and k < half:
            s = half - 1 - k
            arrived(plus_in.at[s], plus_sems.at[1, s])
            total += plus_in[s].astype(F32)
        if k <= 0 and -k < half - 1:
            s = half - 2 + k
            arrived(minus_in.at[s], minus_sems.at[1, s])
            total += minus_in[s].astype(F32)
        if k > 0:
            s = half - k
            plus_out[s] = total.astype(BF16)
            send(plus_out.at[s], plus_in.at[s], plus_sems.at[0, s], plus_sems.at[1, s], device(dz=STRIDE))
        if k < 0:
            s = half - 1 + k
            minus_out[s] = total.astype(BF16)
            send(minus_out.at[s], minus_in.at[s], minus_sems.at[0, s], minus_sems.at[1, s], device(dz=-STRIDE))
        return total

    for j in range(members + 1):
        if j < members:
            over_y(j)
        if j >= 1:
            gradient = over_ring(j - 1)

    new = adam_update(state[0], state[1], state[2], gradient, second_step)
    first = group == 0
    for i in range(3):
        state[i] = new[i]
        top, bottom = state[i, 0:tile, :], state[i, tile:rows, :]
        tile_out[i] = jnp.where(first, bottom, top)
    send(tile_out, tile_in, tile_sems.at[0], tile_sems.at[1], y_peers[2])
    arrived(tile_in, tile_sems.at[1])
    for i, ref in enumerate((master_out, moment_out, variance_out)):
        top, bottom = state[i, 0:tile, :], state[i, tile:rows, :]
        kept = jnp.where(first, top, bottom)
        ref[:, 0:LANES] = jnp.where(first, kept, tile_in[i])
        ref[:, LANES : 2 * LANES] = jnp.where(first, tile_in[i], kept)
    for copy in pending:
        copy.wait_send()


def solution(mesh):
    dp_size = mesh.shape["dp"]
    depth = dp_size // 4
    members = depth // STRIDE
    half = members // 2

    def local(tokens, cotangent, counts, old_offsets, old_master, old_moment, old_variance, old_grad):
        token_rows, width = tokens.shape
        window_rows = old_master.shape[-1] // LANES
        rows = width // dp_size
        margin = (window_rows - rows) // 2
        tile = rows // 2
        out = jax.ShapeDtypeStruct((tile, 2 * LANES), F32)
        piece = (rows, LANES)
        vmem = pl.BlockSpec(memory_space=pltpu.VMEM)
        smem = pl.BlockSpec(memory_space=pltpu.SMEM)
        dma = pltpu.SemaphoreType.DMA
        return pl.pallas_call(
            functools.partial(kernel, dp_size),
            out_shape=(jax.ShapeDtypeStruct(cotangent.shape, BF16), out, out, out),
            in_specs=[smem, smem, pl.BlockSpec(memory_space=pl.ANY)] + [vmem] * 5,
            out_specs=(vmem,) * 4,
            scratch_shapes=[
                pltpu.VMEM((token_rows, width), BF16),
                pltpu.VMEM((width, token_rows), BF16),
                pltpu.VMEM((4, window_rows, LANES), F32),
                pltpu.VMEM((3, window_rows, LANES), F32),
                pltpu.VMEM((2, 3, margin, LANES), F32),
                pltpu.VMEM((2, 3, margin, LANES), F32),
                pltpu.VMEM((3, *piece), F32),
                pltpu.VMEM((2, 2, 2, depth, *piece), BF16),
                pltpu.VMEM((width, 2 * LANES), BF16),
                pltpu.VMEM((2, members, 2, 2, STRIDE, *piece), BF16),
                pltpu.VMEM((members, 2, 2, STRIDE, *piece), BF16),
                pltpu.VMEM((3, members, STRIDE, *piece), BF16),
                pltpu.VMEM((members, STRIDE, *piece), BF16),
                pltpu.VMEM((3, members, *piece), BF16),
                pltpu.VMEM((half, *piece), BF16),
                pltpu.VMEM((half, *piece), BF16),
                pltpu.VMEM((half, *piece), BF16),
                pltpu.VMEM((half, *piece), BF16),
                pltpu.VMEM((3, tile, LANES), F32),
                pltpu.VMEM((3, tile, LANES), F32),
                dma(()),
                dma((4,)),
                dma((2 * half,)),
                dma((depth,)),
                dma((3, members)),
                dma((3, members)),
                dma((3, members)),
                dma((4,)),
                dma((4,)),
                dma((members,)),
                dma((members,)),
                dma((3, members)),
                dma((3, members)),
                dma((3, members)),
                dma((3, members)),
                dma((2, half)),
                dma((2, half)),
                dma((2,)),
            ],
            compiler_params=pltpu.CompilerParams(collective_id=0, has_side_effects=True),
        )(old_offsets, counts, tokens, cotangent, old_master, old_moment, old_variance, old_grad)

    state_spec = P(("tensor", "group"), "dp", None)
    row_spec = P(("dp", "group"), "tensor")
    return jax.shard_map(
        local,
        mesh=mesh,
        in_specs=(P(("dp", "group"), None), row_spec, P(), P(), state_spec, state_spec, state_spec, state_spec),
        out_specs=(row_spec,) * 4,
        check_vma=False,
    )
```

```python
import functools

import jax
import jax.numpy as jnp
from jax import lax
from jax.experimental import pallas as pl
from jax.experimental.pallas import tpu as pltpu
from jax.sharding import PartitionSpec as P

MESH = pl.DeviceIdType.MESH
F32 = jnp.float32
BF16 = jnp.bfloat16

beta_one = 0.9
beta_two = 0.95
epsilon = 1e-08
learn_rate = 0.001
weight_decay = 0.1
first_step = 3.0
second_step = 4.0

LANES = 128
IN_FLIGHT = 2
STRIDE = 4


def adam_update(master, moment, variance, gradient, step_count):
    moment = beta_one * moment + (1.0 - beta_one) * gradient
    variance = beta_two * variance + (1.0 - beta_two) * gradient * gradient
    fix_one = 1.0 - beta_one**step_count
    fix_two = 1.0 - beta_two**step_count
    update = moment / fix_one / (jnp.sqrt(variance / fix_two) + epsilon) + weight_decay * master
    return (master - learn_rate * update, moment, variance)


def kernel(
    dp_size,
    offsets_hbm,
    counts_hbm,
    tok_hbm,
    cot_hbm,
    old_master,
    old_moment,
    old_variance,
    old_grad,
    act_out,
    state_out,
    offsets,
    counts,
    cot,
    flat_old,
    tok,
    tok_t,
    old,
    live_state,
    edge_out,
    edge_in,
    state,
    w,
    w_flat,
    parts,
    core_in,
    y_in,
    z_sum,
    near_in,
    plus_out,
    plus_in,
    minus_out,
    minus_in,
    tile_out,
    tile_in,
    in_sems,
    edge_sems,
    ring_send,
    z_recv,
    near_send,
    y_send,
    y_recv,
    core_send,
    core_recv,
    part_send,
    part_recv,
    sum_send,
    sum_recv,
    window_send,
    window_recv,
    plus_sems,
    minus_sems,
    tile_sems,
):
    depth = dp_size // 4
    members = depth // STRIDE
    half = members // 2
    rows = state.shape[1]
    window_rows = old.shape[1]
    margin = (window_rows - rows) // 2
    tile = rows // 2

    dp = lax.axis_index("dp")
    group = lax.axis_index("group")
    tensor = lax.axis_index("tensor")
    core = lax.rem(dp, 2)
    z = lax.rem(lax.div(dp, 2), depth)
    y_lo = lax.div(dp, 2 * depth)

    def device(dz=0, flip_lo=0, flip_group=0, flip_core=0):
        to_z = lax.rem(z + dz + depth, depth)
        to_lo = 1 - y_lo if flip_lo else y_lo
        to_core = 1 - core if flip_core else core
        to_group = 1 - group if flip_group else group
        return {"dp": (to_lo * depth + to_z) * 2 + to_core, "group": to_group}

    right = {"dp": lax.rem(dp + 1, dp_size), "group": group}
    left = {"dp": lax.rem(dp + dp_size - 1, dp_size), "group": group}
    other_core = device(flip_core=1)
    y_flips = ((1, 0), (1, 1), (0, 1))
    y_peers = [device(flip_lo=l, flip_group=g) for l, g in y_flips]

    def remote(src, dst, send_sem, recv_sem, to):
        return pltpu.make_async_remote_copy(
            src_ref=src,
            dst_ref=dst,
            send_sem=send_sem,
            recv_sem=recv_sem,
            device_id=to,
            device_id_type=MESH,
        )

    pending = []

    def send(src, dst, send_sem, recv_sem, to):
        copy = remote(src, dst, send_sem, recv_sem, to)
        copy.start()
        pending.append(copy)

    def arrived(dst, recv_sem):
        remote(dst, dst, recv_sem, recv_sem, other_core).wait_recv()

    olds = (old_master, old_moment, old_variance, old_grad)
    copies = [pltpu.make_async_copy(ref.at[0], flat_old.at[i], in_sems.at[i]) for i, ref in enumerate(olds)]
    copies.append(pltpu.make_async_copy(offsets_hbm, offsets, in_sems.at[4]))
    late = [
        pltpu.make_async_copy(tok_hbm, tok, in_sems.at[5]),
        pltpu.make_async_copy(cot_hbm, cot, in_sems.at[6]),
        pltpu.make_async_copy(counts_hbm, counts, in_sems.at[7]),
    ]
    for copy in copies + late:
        copy.start()

    barrier = pltpu.get_barrier_semaphore()
    greeted = [right, left, other_core, *y_peers]
    greeted += [device(dz=d) for d in (STRIDE, -STRIDE, 1, -1, 2, -2)]
    for peer in greeted:
        pl.semaphore_signal(barrier, inc=1, device_id=peer, device_id_type=MESH)

    for copy in copies:
        copy.wait()
    for r in range(window_rows):
        lanes = slice(r * LANES, (r + 1) * LANES)
        for i in range(4):
            old[i, r : r + 1, :] = flat_old[i, :, lanes]
    updated = adam_update(old[0], old[1], old[2], old[3], first_step)
    shape = (window_rows, LANES)
    position = (
        dp * (rows * LANES)
        - margin * LANES
        + lax.broadcasted_iota(jnp.int32, shape, 0) * LANES
        + lax.broadcasted_iota(jnp.int32, shape, 1)
    )
    slab = tensor * 2 + group
    low, high = offsets[slab, dp], offsets[slab, dp + 1]
    is_live = (position >= low) & (position < high)
    for i in range(3):
        live_state[i] = jnp.where(is_live, updated[i], F32(0.0))
    for i in range(3):
        edge_out[0, i] = live_state[i, rows + margin : window_rows, :]
        edge_out[1, i] = live_state[i, 0:margin, :]
    pl.semaphore_wait(barrier, len(greeted))
    send(edge_out.at[0], edge_in.at[0], edge_sems.at[0], edge_sems.at[2], right)
    send(edge_out.at[1], edge_in.at[1], edge_sems.at[1], edge_sems.at[3], left)
    for i in range(3):
        state[i] = live_state[i, margin : margin + rows, :]
    arrived(edge_in.at[0], edge_sems.at[2])
    arrived(edge_in.at[1], edge_sems.at[3])
    for i in range(3):
        state[i, 0:margin, :] += edge_in[0, i]
        state[i, rows - margin : rows, :] += edge_in[1, i]

    line = w.at[group, y_lo, core]
    base = STRIDE * (half - 1) + 1

    def ring(k, direction):
        to = k - direction
        to = half if to == -half else to
        src, dst = base + STRIDE * k, base + STRIDE * to
        index = -k if direction > 0 else half + k
        send(line.at[src], line.at[dst], ring_send.at[index], z_recv.at[dst], device(dz=direction * STRIDE))

    def near(k):
        src = base + STRIDE * k
        for i, d in enumerate((-1, 1, -2)):
            send(line.at[src], line.at[src - d], near_send.at[i, k + half - 1], z_recv.at[src - d], device(dz=d))

    def along_y(k):
        block = k + half - 1
        for d in (-1, 1, 2):
            slot = base + STRIDE * k + d
            arrived(line.at[slot], z_recv.at[slot])
        piece = line.at[pl.ds(block * STRIDE, STRIDE)]
        for i, peer in enumerate(y_peers):
            send(piece, piece, y_send.at[i, block], y_recv.at[i, block], peer)

    def from_ring(k):
        slot = base + STRIDE * k
        arrived(line.at[slot], z_recv.at[slot])

    line[base] = state[0].astype(BF16)
    ring(0, 1)
    ring(0, -1)
    near(0)

    for copy in late:
        copy.wait()
    low_slot = STRIDE * (half - 1) + 2
    group_z = 8
    group_rows = group_z * 2 * rows

    def transpose(i, carry):
        columns = tok[:, pl.ds(pl.multiple_of(i * group_rows, group_rows), group_rows)].T
        for n in range(group_z):
            nat = i * group_z + n
            lo = lax.div(nat, depth)
            slot = lax.rem(lax.rem(nat, depth) - z + low_slot + depth, depth)
            start = pl.multiple_of((lo * depth + slot) * (2 * rows), 2 * rows)
            tok_t[pl.ds(start, 2 * rows), :] = columns[n * 2 * rows : (n + 1) * 2 * rows, :]
        return carry

    lax.fori_loop(0, 2 * depth // group_z, transpose, 0)

    for k in range(1, half):
        from_ring(-k)
        ring(-k, 1)
        near(-k)
        from_ring(k)
        if k < half - 1:
            ring(k, -1)
        near(k)
        along_y(1 - k)
        if k > 1:
            along_y(k - 1)
    from_ring(half)
    near(half)
    along_y(1 - half)
    along_y(half - 1)
    along_y(half)

    def to_core(i, lo, g):
        src = w.at[g, lo, core]
        send(src, src, core_send.at[i], core_recv.at[i], other_core)

    def lines(i):
        l, g = ((0, 0),) [0] if i == 0 else y_flips[i - 1]
        return (1 - y_lo if l else y_lo), (1 - group if g else group)

    to_core(0, y_lo, group)
    for i in range(3):
        lo, g = lines(i + 1)
        for block in range(members):
            src = w.at[g, lo, core, pl.ds(block * STRIDE, STRIDE)]
            arrived(src, y_recv.at[i, block])
        to_core(i + 1, lo, g)
    for i in range(4):
        lo, g = lines(i)
        arrived(w.at[g, lo, 1 - core], core_recv.at[i])

    def flatten(zz, carry):
        for lo in range(2):
            to_z = lax.rem(z + zz - base + depth, depth)
            start = pl.multiple_of((lo * depth + to_z) * (2 * rows), 2 * rows)
            for g in range(2):
                both = jnp.concatenate([w[g, lo, 0, zz], w[g, lo, 1, zz]], axis=0)
                w_flat[pl.ds(start, 2 * rows), g * LANES : (g + 1) * LANES] = both
        return carry

    lax.fori_loop(0, depth, flatten, 0)
    preact = jnp.dot(tok[...], w_flat[...], preferred_element_type=F32)
    sigmoid_z = jax.nn.sigmoid(preact)
    act_out[...] = (preact * sigmoid_z).astype(BF16)
    derivative = sigmoid_z * (1.0 + preact * (1.0 - sigmoid_z))
    my_count = counts[dp * 2 + group]
    row_live = lax.broadcasted_iota(jnp.int32, preact.shape, 0) < my_count
    delta = jnp.where(row_live, cot[...].astype(F32) * derivative, F32(0.0)).astype(BF16)

    order = [half] + [s * k for k in range(half - 1, 0, -1) for s in (1, -1)] + [0]
    blocks = [k + half - 1 for k in order]
    for block in blocks:
        for lo in range(2):
            count = STRIDE * 2 * rows
            start = (lo * depth + block * STRIDE) * (2 * rows)
            part = jnp.dot(tok_t[pl.ds(start, count), :], delta, preferred_element_type=F32)
            for zz in range(STRIDE):
                for c in range(2):
                    top = (zz * 2 + c) * rows
                    for g in range(2):
                        parts[c, block, g, lo, zz] = part[top : top + rows, g * LANES : (g + 1) * LANES].astype(BF16)
        send(parts.at[1 - core, block], core_in.at[block], part_send.at[block], part_recv.at[block], other_core)
    def over_core(j):
        block = blocks[j]
        arrived(core_in.at[block], part_recv.at[block])
        both = parts[core, block].astype(F32) + core_in[block].astype(F32)
        parts[core, block] = both.astype(BF16)
        for i, (l, g) in enumerate(y_flips):
            lo = 1 - y_lo if l else y_lo
            gg = 1 - group if g else group
            send(parts.at[core, block, gg, lo], y_in.at[i, block], sum_send.at[i, block], sum_recv.at[i, block], y_peers[i])

    def over_y(j):
        block = blocks[j]
        total = parts[core, block, group, y_lo].astype(F32)
        for i in range(3):
            arrived(y_in.at[i, block], sum_recv.at[i, block])
            total += y_in[i, block].astype(F32)
        z_sum[block] = total.astype(BF16)
        for i, dz in enumerate((-2, -1, 1)):
            src = z_sum.at[block, 2 + dz]
            send(src, near_in.at[i, block], window_send.at[i, block], window_recv.at[i, block], device(dz=dz))

    def over_ring(j):
        block, k = blocks[j], order[j]
        total = z_sum[block, 2].astype(F32)
        for i in range(3):
            arrived(near_in.at[i, block], window_recv.at[i, block])
            total += near_in[i, block].astype(F32)
        if k >= 0 and k < half:
            s = half - 1 - k
            arrived(plus_in.at[s], plus_sems.at[1, s])
            total += plus_in[s].astype(F32)
        if k <= 0 and -k < half - 1:
            s = half - 2 + k
            arrived(minus_in.at[s], minus_sems.at[1, s])
            total += minus_in[s].astype(F32)
        if k > 0:
            s = half - k
            plus_out[s] = total.astype(BF16)
            send(plus_out.at[s], plus_in.at[s], plus_sems.at[0, s], plus_sems.at[1, s], device(dz=STRIDE))
        if k < 0:
            s = half - 1 + k
            minus_out[s] = total.astype(BF16)
            send(minus_out.at[s], minus_in.at[s], minus_sems.at[0, s], minus_sems.at[1, s], device(dz=-STRIDE))
        return total

    for j in range(IN_FLIGHT):
        over_core(j)
    for j in range(members + 1):
        if j < members:
            over_y(j)
        if j + IN_FLIGHT < members:
            over_core(j + IN_FLIGHT)
        if j >= 1:
            gradient = over_ring(j - 1)

    new = adam_update(state[0], state[1], state[2], gradient, second_step)
    first = group == 0
    for i in range(3):
        state[i] = new[i]
        top, bottom = state[i, 0:tile, :], state[i, tile:rows, :]
        tile_out[i] = jnp.where(first, bottom, top)
    send(tile_out, tile_in, tile_sems.at[0], tile_sems.at[1], y_peers[2])
    arrived(tile_in, tile_sems.at[1])
    for i in range(3):
        top, bottom = state[i, 0:tile, :], state[i, tile:rows, :]
        kept = jnp.where(first, top, bottom)
        state_out[i, :, 0:LANES] = jnp.where(first, kept, tile_in[i])
        state_out[i, :, LANES : 2 * LANES] = jnp.where(first, tile_in[i], kept)
    for copy in pending:
        copy.wait_send()


def finish(act, state, act_out, master_out, moment_out, variance_out):
    act_out[...] = act[...]
    for i, ref in enumerate((master_out, moment_out, variance_out)):
        ref[...] = state[i]


def solution(mesh):
    dp_size = mesh.shape["dp"]
    depth = dp_size // 4
    members = depth // STRIDE
    half = members // 2

    def local(tokens, cotangent, counts, old_offsets, old_master, old_moment, old_variance, old_grad):
        token_rows, width = tokens.shape
        window_rows = old_master.shape[-1] // LANES
        rows = width // dp_size
        margin = (window_rows - rows) // 2
        tile = rows // 2
        out = jax.ShapeDtypeStruct((tile, 2 * LANES), F32)
        piece = (rows, LANES)
        vmem = pl.BlockSpec(memory_space=pltpu.VMEM)
        dma = pltpu.SemaphoreType.DMA
        act_shape = jax.ShapeDtypeStruct(cotangent.shape, BF16)
        act, new_state = pl.pallas_call(
            functools.partial(kernel, dp_size),
            out_shape=(act_shape, jax.ShapeDtypeStruct((3, tile, 2 * LANES), F32)),
            in_specs=[pl.BlockSpec(memory_space=pltpu.HBM)] * 8,
            out_specs=(vmem,) * 2,
            scratch_shapes=[
                pltpu.SMEM(old_offsets.shape, jnp.int32),
                pltpu.SMEM(counts.shape, jnp.int32),
                pltpu.VMEM(cotangent.shape, BF16),
                pltpu.VMEM((4, 1, old_master.shape[-1]), F32),
                pltpu.VMEM((token_rows, width), BF16),
                pltpu.VMEM((width, token_rows), BF16),
                pltpu.VMEM((4, window_rows, LANES), F32),
                pltpu.VMEM((3, window_rows, LANES), F32),
                pltpu.VMEM((2, 3, margin, LANES), F32),
                pltpu.VMEM((2, 3, margin, LANES), F32),
                pltpu.VMEM((3, *piece), F32),
                pltpu.VMEM((2, 2, 2, depth, *piece), BF16),
                pltpu.VMEM((width, 2 * LANES), BF16),
                pltpu.VMEM((2, members, 2, 2, STRIDE, *piece), BF16),
                pltpu.VMEM((members, 2, 2, STRIDE, *piece), BF16),
                pltpu.VMEM((3, members, STRIDE, *piece), BF16),
                pltpu.VMEM((members, STRIDE, *piece), BF16),
                pltpu.VMEM((3, members, *piece), BF16),
                pltpu.VMEM((half, *piece), BF16),
                pltpu.VMEM((half, *piece), BF16),
                pltpu.VMEM((half, *piece), BF16),
                pltpu.VMEM((half, *piece), BF16),
                pltpu.VMEM((3, tile, LANES), F32),
                pltpu.VMEM((3, tile, LANES), F32),
                dma((8,)),
                dma((4,)),
                dma((2 * half,)),
                dma((depth,)),
                dma((3, members)),
                dma((3, members)),
                dma((3, members)),
                dma((4,)),
                dma((4,)),
                dma((members,)),
                dma((members,)),
                dma((3, members)),
                dma((3, members)),
                dma((3, members)),
                dma((3, members)),
                dma((2, half)),
                dma((2, half)),
                dma((2,)),
            ],
            compiler_params=pltpu.CompilerParams(
                collective_id=0, has_side_effects=True, vmem_limit_bytes=60 * 1024 * 1024
            ),
        )(old_offsets, counts, tokens, cotangent, old_master, old_moment, old_variance, old_grad)
        return pl.pallas_call(
            finish,
            out_shape=(act_shape, out, out, out),
            in_specs=[vmem] * 2,
            out_specs=(vmem,) * 4,
        )(act, new_state)

    state_spec = P(("tensor", "group"), "dp", None)
    row_spec = P(("dp", "group"), "tensor")
    return jax.shard_map(
        local,
        mesh=mesh,
        in_specs=(P(("dp", "group"), None), row_spec, P(), P(), state_spec, state_spec, state_spec, state_spec),
        out_specs=(row_spec,) * 4,
        check_vma=False,
    )
```

```python
import functools

import jax
import jax.numpy as jnp
from jax import lax
from jax.experimental import pallas as pl
from jax.experimental.pallas import tpu as pltpu
from jax.sharding import PartitionSpec as P

MESH = pl.DeviceIdType.MESH
F32 = jnp.float32
BF16 = jnp.bfloat16

beta_one = 0.9
beta_two = 0.95
epsilon = 1e-08
learn_rate = 0.001
weight_decay = 0.1
first_step = 3.0
second_step = 4.0

LANES = 128
IN_FLIGHT = 2
STRIDE = 4


def adam_update(master, moment, variance, gradient, step_count):
    moment = beta_one * moment + (1.0 - beta_one) * gradient
    variance = beta_two * variance + (1.0 - beta_two) * gradient * gradient
    fix_one = 1.0 - beta_one**step_count
    fix_two = 1.0 - beta_two**step_count
    update = moment / fix_one / (jnp.sqrt(variance / fix_two) + epsilon) + weight_decay * master
    return (master - learn_rate * update, moment, variance)


def kernel(
    dp_size,
    offsets_hbm,
    counts_hbm,
    tok_hbm,
    cot_hbm,
    old_master,
    old_moment,
    old_variance,
    old_grad,
    act_out,
    state_out,
    offsets,
    counts,
    cot,
    flat_old,
    tok,
    tok_t,
    old,
    live_state,
    edge_out,
    edge_in,
    state,
    w,
    w_flat,
    parts,
    core_in,
    y_in,
    z_sum,
    near_in,
    plus_out,
    plus_in,
    minus_out,
    minus_in,
    tile_out,
    tile_in,
    kept,
    ends,
    ends_out,
    ends_in,
    act,
    in_sems,
    edge_sems,
    ring_send,
    z_recv,
    near_send,
    y_send,
    y_recv,
    core_send,
    core_recv,
    part_send,
    part_recv,
    sum_send,
    sum_recv,
    window_send,
    window_recv,
    plus_sems,
    minus_sems,
    tile_sems,
    end_sems,
    act_sem,
):
    depth = dp_size // 4
    members = depth // STRIDE
    half = members // 2
    rows = state.shape[1]
    window_rows = old.shape[1]
    margin = (window_rows - rows) // 2
    tile = rows // 2

    dp = lax.axis_index("dp")
    group = lax.axis_index("group")
    tensor = lax.axis_index("tensor")
    core = lax.rem(dp, 2)
    z = lax.rem(lax.div(dp, 2), depth)
    y_lo = lax.div(dp, 2 * depth)

    def device(dz=0, flip_lo=0, flip_group=0, flip_core=0):
        to_z = lax.rem(z + dz + depth, depth)
        to_lo = 1 - y_lo if flip_lo else y_lo
        to_core = 1 - core if flip_core else core
        to_group = 1 - group if flip_group else group
        return {"dp": (to_lo * depth + to_z) * 2 + to_core, "group": to_group}

    right = {"dp": lax.rem(dp + 1, dp_size), "group": group}
    left = {"dp": lax.rem(dp + dp_size - 1, dp_size), "group": group}
    other_core = device(flip_core=1)
    y_flips = ((1, 0), (1, 1), (0, 1))
    y_peers = [device(flip_lo=l, flip_group=g) for l, g in y_flips]

    def remote(src, dst, send_sem, recv_sem, to):
        return pltpu.make_async_remote_copy(
            src_ref=src,
            dst_ref=dst,
            send_sem=send_sem,
            recv_sem=recv_sem,
            device_id=to,
            device_id_type=MESH,
        )

    pending = []

    def send(src, dst, send_sem, recv_sem, to):
        copy = remote(src, dst, send_sem, recv_sem, to)
        copy.start()
        pending.append(copy)

    def arrived(dst, recv_sem):
        remote(dst, dst, recv_sem, recv_sem, other_core).wait_recv()

    olds = (old_master, old_moment, old_variance, old_grad)
    copies = [pltpu.make_async_copy(ref.at[0], flat_old.at[i], in_sems.at[i]) for i, ref in enumerate(olds)]
    copies.append(pltpu.make_async_copy(offsets_hbm, offsets, in_sems.at[4]))
    late = [
        pltpu.make_async_copy(tok_hbm, tok, in_sems.at[5]),
        pltpu.make_async_copy(cot_hbm, cot, in_sems.at[6]),
        pltpu.make_async_copy(counts_hbm, counts, in_sems.at[7]),
    ]
    for copy in copies + late:
        copy.start()

    barrier = pltpu.get_barrier_semaphore()
    greeted = [right, left, other_core, *y_peers]
    greeted += [device(dz=d) for d in (STRIDE, -STRIDE, 1, -1, 2, -2)]
    greeted += [device(dz=d, flip_group=1) for d in (STRIDE, -STRIDE)]
    for peer in greeted:
        pl.semaphore_signal(barrier, inc=1, device_id=peer, device_id_type=MESH)

    for copy in copies:
        copy.wait()
    for r in range(window_rows):
        lanes = slice(r * LANES, (r + 1) * LANES)
        for i in range(4):
            old[i, r : r + 1, :] = flat_old[i, :, lanes]
    updated = adam_update(old[0], old[1], old[2], old[3], first_step)
    shape = (window_rows, LANES)
    position = (
        dp * (rows * LANES)
        - margin * LANES
        + lax.broadcasted_iota(jnp.int32, shape, 0) * LANES
        + lax.broadcasted_iota(jnp.int32, shape, 1)
    )
    slab = tensor * 2 + group
    low, high = offsets[slab, dp], offsets[slab, dp + 1]
    is_live = (position >= low) & (position < high)
    for i in range(3):
        live_state[i] = jnp.where(is_live, updated[i], F32(0.0))
    for i in range(3):
        edge_out[0, i] = live_state[i, rows + margin : window_rows, :]
        edge_out[1, i] = live_state[i, 0:margin, :]
    pl.semaphore_wait(barrier, len(greeted))
    send(edge_out.at[0], edge_in.at[0], edge_sems.at[0], edge_sems.at[2], right)
    send(edge_out.at[1], edge_in.at[1], edge_sems.at[1], edge_sems.at[3], left)
    for i in range(3):
        state[i] = live_state[i, margin : margin + rows, :]
    arrived(edge_in.at[0], edge_sems.at[2])
    arrived(edge_in.at[1], edge_sems.at[3])
    for i in range(3):
        state[i, 0:margin, :] += edge_in[0, i]
        state[i, rows - margin : rows, :] += edge_in[1, i]

    first = group == 0
    for i in range(3):
        top, bottom = state[i, 0:tile, :], state[i, tile:rows, :]
        tile_out[i] = jnp.where(first, bottom, top)
        kept[i] = jnp.where(first, top, bottom)

    line = w.at[group, y_lo, core]
    base = STRIDE * (half - 1) + 1

    def ring(k, direction):
        to = k - direction
        to = half if to == -half else to
        src, dst = base + STRIDE * k, base + STRIDE * to
        index = -k if direction > 0 else half + k
        send(line.at[src], line.at[dst], ring_send.at[index], z_recv.at[dst], device(dz=direction * STRIDE))

    def near(k):
        src = base + STRIDE * k
        for i, d in enumerate((-1, 1, -2)):
            send(line.at[src], line.at[src - d], near_send.at[i, k + half - 1], z_recv.at[src - d], device(dz=d))

    def along_y(k):
        block = k + half - 1
        for d in (-1, 1, 2):
            slot = base + STRIDE * k + d
            arrived(line.at[slot], z_recv.at[slot])
        piece = line.at[pl.ds(block * STRIDE, STRIDE)]
        for i, peer in enumerate(y_peers):
            send(piece, piece, y_send.at[i, block], y_recv.at[i, block], peer)

    def from_ring(k):
        slot = base + STRIDE * k
        arrived(line.at[slot], z_recv.at[slot])

    line[base] = state[0].astype(BF16)
    ring(0, 1)
    ring(0, -1)
    near(0)

    partner = y_peers[2]
    send(tile_out, tile_in, tile_sems.at[0], tile_sems.at[1], partner)

    for copy in late:
        copy.wait()
    low_slot = STRIDE * (half - 1) + 2
    group_z = 8
    group_rows = group_z * 2 * rows

    def transpose(i, carry):
        columns = tok[:, pl.ds(pl.multiple_of(i * group_rows, group_rows), group_rows)].T
        for n in range(group_z):
            nat = i * group_z + n
            lo = lax.div(nat, depth)
            slot = lax.rem(lax.rem(nat, depth) - z + low_slot + depth, depth)
            start = pl.multiple_of((lo * depth + slot) * (2 * rows), 2 * rows)
            tok_t[pl.ds(start, 2 * rows), :] = columns[n * 2 * rows : (n + 1) * 2 * rows, :]
        return carry

    lax.fori_loop(0, 2 * depth // group_z, transpose, 0)

    for k in range(1, half):
        from_ring(-k)
        ring(-k, 1)
        near(-k)
        from_ring(k)
        if k < half - 1:
            ring(k, -1)
        near(k)
        along_y(1 - k)
        if k > 1:
            along_y(k - 1)
    from_ring(half)
    near(half)
    along_y(1 - half)
    along_y(half - 1)
    along_y(half)

    def to_core(i, lo, g):
        src = w.at[g, lo, core]
        send(src, src, core_send.at[i], core_recv.at[i], other_core)

    def lines(i):
        l, g = ((0, 0),) [0] if i == 0 else y_flips[i - 1]
        return (1 - y_lo if l else y_lo), (1 - group if g else group)

    to_core(0, y_lo, group)
    for i in range(3):
        lo, g = lines(i + 1)
        for block in range(members):
            src = w.at[g, lo, core, pl.ds(block * STRIDE, STRIDE)]
            arrived(src, y_recv.at[i, block])
        to_core(i + 1, lo, g)
    for i in range(4):
        lo, g = lines(i)
        arrived(w.at[g, lo, 1 - core], core_recv.at[i])

    def flatten(zz, carry):
        for lo in range(2):
            to_z = lax.rem(z + zz - base + depth, depth)
            start = pl.multiple_of((lo * depth + to_z) * (2 * rows), 2 * rows)
            for g in range(2):
                both = jnp.concatenate([w[g, lo, 0, zz], w[g, lo, 1, zz]], axis=0)
                w_flat[pl.ds(start, 2 * rows), g * LANES : (g + 1) * LANES] = both
        return carry

    lax.fori_loop(0, depth, flatten, 0)
    preact = jnp.dot(tok[...], w_flat[...], preferred_element_type=F32)
    sigmoid_z = jax.nn.sigmoid(preact)
    act[...] = (preact * sigmoid_z).astype(BF16)
    act_copy = pltpu.make_async_copy(act, act_out, act_sem)
    act_copy.start()
    derivative = sigmoid_z * (1.0 + preact * (1.0 - sigmoid_z))
    my_count = counts[dp * 2 + group]
    row_live = lax.broadcasted_iota(jnp.int32, preact.shape, 0) < my_count
    delta = jnp.where(row_live, cot[...].astype(F32) * derivative, F32(0.0)).astype(BF16)

    order = [half] + [s * k for k in range(half - 1, 0, -1) for s in (1, -1)] + [0]
    blocks = [k + half - 1 for k in order]
    for block in blocks:
        for lo in range(2):
            count = STRIDE * 2 * rows
            start = (lo * depth + block * STRIDE) * (2 * rows)
            part = jnp.dot(tok_t[pl.ds(start, count), :], delta, preferred_element_type=F32)
            for zz in range(STRIDE):
                for c in range(2):
                    top = (zz * 2 + c) * rows
                    for g in range(2):
                        parts[c, block, g, lo, zz] = part[top : top + rows, g * LANES : (g + 1) * LANES].astype(BF16)
        send(parts.at[1 - core, block], core_in.at[block], part_send.at[block], part_recv.at[block], other_core)
    def over_core(j):
        block = blocks[j]
        arrived(core_in.at[block], part_recv.at[block])
        both = parts[core, block].astype(F32) + core_in[block].astype(F32)
        parts[core, block] = both.astype(BF16)
        for i, (l, g) in enumerate(y_flips):
            lo = 1 - y_lo if l else y_lo
            gg = 1 - group if g else group
            send(parts.at[core, block, gg, lo], y_in.at[i, block], sum_send.at[i, block], sum_recv.at[i, block], y_peers[i])

    def over_y(j):
        block = blocks[j]
        total = parts[core, block, group, y_lo].astype(F32)
        for i in range(3):
            arrived(y_in.at[i, block], sum_recv.at[i, block])
            total += y_in[i, block].astype(F32)
        z_sum[block] = total.astype(BF16)
        for i, dz in enumerate((-2, -1, 1)):
            src = z_sum.at[block, 2 + dz]
            send(src, near_in.at[i, block], window_send.at[i, block], window_recv.at[i, block], device(dz=dz))

    def halves(i, total, dz):
        ends[i, 0] = total[0:tile]
        ends[i, 1] = total[tile:rows]
        ends_out[i] = ends[i].astype(BF16)
        for own, to in ((1, device(dz=dz)), (0, device(dz=dz, flip_group=1))):
            if own and dz == 0:
                continue
            half_rows = group if own else 1 - group
            n = 4 if dz == 0 else 2 * i + 1 - own
            send(ends_out.at[i, half_rows], ends_in.at[n], end_sems.at[0, n], end_sems.at[1, n], to)

    def over_ring(j):
        block, k = blocks[j], order[j]
        total = z_sum[block, 2].astype(F32)
        for i in range(3):
            arrived(near_in.at[i, block], window_recv.at[i, block])
            total += near_in[i, block].astype(F32)
        if k == 0:
            halves(2, total, 0)
            own_sum = jnp.where(first, total[0:tile], total[tile:rows])
            for n in range(5):
                arrived(ends_in.at[n], end_sems.at[1, n])
            mine = own_sum + ends_in[0].astype(F32) + ends_in[2].astype(F32)
            theirs = ends_in[1].astype(F32) + ends_in[3].astype(F32) + ends_in[4].astype(F32)
            return mine, theirs
        if k >= 0 and k < half:
            s = half - 1 - k
            arrived(plus_in.at[s], plus_sems.at[1, s])
            total += plus_in[s].astype(F32)
        if k <= 0 and -k < half - 1:
            s = half - 2 + k
            arrived(minus_in.at[s], minus_sems.at[1, s])
            total += minus_in[s].astype(F32)
        if k == 1 or k == -1:
            halves(0 if k > 0 else 1, total, STRIDE * k)
        elif k > 0:
            s = half - k
            plus_out[s] = total.astype(BF16)
            send(plus_out.at[s], plus_in.at[s], plus_sems.at[0, s], plus_sems.at[1, s], device(dz=STRIDE))
        elif k < 0:
            s = half - 1 + k
            minus_out[s] = total.astype(BF16)
            send(minus_out.at[s], minus_in.at[s], minus_sems.at[0, s], minus_sems.at[1, s], device(dz=-STRIDE))
        return total

    for j in range(IN_FLIGHT):
        over_core(j)
    for j in range(members + 1):
        if j < members:
            over_y(j)
        if j + IN_FLIGHT < members:
            over_core(j + IN_FLIGHT)
        if j >= 1:
            gradient = over_ring(j - 1)

    arrived(tile_in, tile_sems.at[1])
    for lanes, old_state, summed in ((group, kept, gradient[0]), (1 - group, tile_in, gradient[1])):
        new = adam_update(old_state[0], old_state[1], old_state[2], summed, second_step)
        start = pl.multiple_of(lanes * LANES, LANES)
        for i in range(3):
            state_out[i, :, pl.ds(start, LANES)] = new[i]
    act_copy.wait()
    for copy in pending:
        copy.wait_send()


def finish(act, state, act_out, master_out, moment_out, variance_out):
    act_out[...] = act[...]
    for i, ref in enumerate((master_out, moment_out, variance_out)):
        ref[...] = state[i]


def solution(mesh):
    dp_size = mesh.shape["dp"]
    depth = dp_size // 4
    members = depth // STRIDE
    half = members // 2

    def local(tokens, cotangent, counts, old_offsets, old_master, old_moment, old_variance, old_grad):
        token_rows, width = tokens.shape
        window_rows = old_master.shape[-1] // LANES
        rows = width // dp_size
        margin = (window_rows - rows) // 2
        tile = rows // 2
        out = jax.ShapeDtypeStruct((tile, 2 * LANES), F32)
        piece = (rows, LANES)
        vmem = pl.BlockSpec(memory_space=pltpu.VMEM)
        dma = pltpu.SemaphoreType.DMA
        act_shape = jax.ShapeDtypeStruct(cotangent.shape, BF16)
        act, new_state = pl.pallas_call(
            functools.partial(kernel, dp_size),
            out_shape=(act_shape, jax.ShapeDtypeStruct((3, tile, 2 * LANES), F32)),
            in_specs=[pl.BlockSpec(memory_space=pltpu.HBM)] * 8,
            out_specs=(pl.BlockSpec(memory_space=pltpu.HBM), vmem),
            scratch_shapes=[
                pltpu.SMEM(old_offsets.shape, jnp.int32),
                pltpu.SMEM(counts.shape, jnp.int32),
                pltpu.VMEM(cotangent.shape, BF16),
                pltpu.VMEM((4, 1, old_master.shape[-1]), F32),
                pltpu.VMEM((token_rows, width), BF16),
                pltpu.VMEM((width, token_rows), BF16),
                pltpu.VMEM((4, window_rows, LANES), F32),
                pltpu.VMEM((3, window_rows, LANES), F32),
                pltpu.VMEM((2, 3, margin, LANES), F32),
                pltpu.VMEM((2, 3, margin, LANES), F32),
                pltpu.VMEM((3, *piece), F32),
                pltpu.VMEM((2, 2, 2, depth, *piece), BF16),
                pltpu.VMEM((width, 2 * LANES), BF16),
                pltpu.VMEM((2, members, 2, 2, STRIDE, *piece), BF16),
                pltpu.VMEM((members, 2, 2, STRIDE, *piece), BF16),
                pltpu.VMEM((3, members, STRIDE, *piece), BF16),
                pltpu.VMEM((members, STRIDE, *piece), BF16),
                pltpu.VMEM((3, members, *piece), BF16),
                pltpu.VMEM((half, *piece), BF16),
                pltpu.VMEM((half, *piece), BF16),
                pltpu.VMEM((half, *piece), BF16),
                pltpu.VMEM((half, *piece), BF16),
                pltpu.VMEM((3, tile, LANES), F32),
                pltpu.VMEM((3, tile, LANES), F32),
                pltpu.VMEM((3, tile, LANES), F32),
                pltpu.VMEM((3, 2, tile, LANES), F32),
                pltpu.VMEM((3, 2, tile, LANES), BF16),
                pltpu.VMEM((5, tile, LANES), BF16),
                pltpu.VMEM(cotangent.shape, BF16),
                dma((8,)),
                dma((4,)),
                dma((2 * half,)),
                dma((depth,)),
                dma((3, members)),
                dma((3, members)),
                dma((3, members)),
                dma((4,)),
                dma((4,)),
                dma((members,)),
                dma((members,)),
                dma((3, members)),
                dma((3, members)),
                dma((3, members)),
                dma((3, members)),
                dma((2, half)),
                dma((2, half)),
                dma((2,)),
                dma((2, 5)),
                dma(()),
            ],
            compiler_params=pltpu.CompilerParams(
                collective_id=0, has_side_effects=True, vmem_limit_bytes=60 * 1024 * 1024
            ),
        )(old_offsets, counts, tokens, cotangent, old_master, old_moment, old_variance, old_grad)
        return pl.pallas_call(
            finish,
            out_shape=(act_shape, out, out, out),
            in_specs=[vmem] * 2,
            out_specs=(vmem,) * 4,
        )(act, new_state)

    state_spec = P(("tensor", "group"), "dp", None)
    row_spec = P(("dp", "group"), "tensor")
    return jax.shard_map(
        local,
        mesh=mesh,
        in_specs=(P(("dp", "group"), None), row_spec, P(), P(), state_spec, state_spec, state_spec, state_spec),
        out_specs=(row_spec,) * 4,
        check_vma=False,
    )
```

```python
import functools

import jax
import jax.numpy as jnp
from jax import lax
from jax.experimental import pallas as pl
from jax.experimental.pallas import tpu as pltpu
from jax.sharding import PartitionSpec as P

MESH = pl.DeviceIdType.MESH
F32 = jnp.float32
BF16 = jnp.bfloat16

beta_one = 0.9
beta_two = 0.95
epsilon = 1e-08
learn_rate = 0.001
weight_decay = 0.1
first_step = 3.0
second_step = 4.0

LANES = 128
IN_FLIGHT = 3
STRIDE = 4


def adam_update(master, moment, variance, gradient, step_count):
    moment = beta_one * moment + (1.0 - beta_one) * gradient
    variance = beta_two * variance + (1.0 - beta_two) * gradient * gradient
    fix_one = 1.0 - beta_one**step_count
    fix_two = 1.0 - beta_two**step_count
    update = moment / fix_one / (jnp.sqrt(variance / fix_two) + epsilon) + weight_decay * master
    return (master - learn_rate * update, moment, variance)


def kernel(
    dp_size,
    offsets_hbm,
    counts_hbm,
    tok_hbm,
    cot_hbm,
    old_master,
    old_moment,
    old_variance,
    old_grad,
    act_out,
    state_out,
    offsets,
    counts,
    cot,
    flat_old,
    tok,
    tok_t,
    old,
    live_state,
    edge_out,
    edge_in,
    state,
    w,
    w_flat,
    parts,
    core_in,
    y_in,
    z_sum,
    near_in,
    plus_out,
    plus_in,
    minus_out,
    minus_in,
    tile_out,
    tile_in,
    kept,
    ends,
    ends_out,
    ends_in,
    act,
    in_sems,
    edge_sems,
    ring_send,
    z_recv,
    near_send,
    y_send,
    y_recv,
    core_send,
    core_recv,
    part_send,
    part_recv,
    sum_send,
    sum_recv,
    window_send,
    window_recv,
    plus_sems,
    minus_sems,
    tile_sems,
    end_sems,
    act_sem,
):
    depth = dp_size // 4
    members = depth // STRIDE
    half = members // 2
    rows = state.shape[1]
    window_rows = old.shape[1]
    margin = (window_rows - rows) // 2
    tile = rows // 2

    dp = lax.axis_index("dp")
    group = lax.axis_index("group")
    tensor = lax.axis_index("tensor")
    core = lax.rem(dp, 2)
    z = lax.rem(lax.div(dp, 2), depth)
    y_lo = lax.div(dp, 2 * depth)

    def device(dz=0, flip_lo=0, flip_group=0, flip_core=0):
        to_z = lax.rem(z + dz + depth, depth)
        to_lo = 1 - y_lo if flip_lo else y_lo
        to_core = 1 - core if flip_core else core
        to_group = 1 - group if flip_group else group
        return {"dp": (to_lo * depth + to_z) * 2 + to_core, "group": to_group}

    right = {"dp": lax.rem(dp + 1, dp_size), "group": group}
    left = {"dp": lax.rem(dp + dp_size - 1, dp_size), "group": group}
    other_core = device(flip_core=1)
    y_flips = ((1, 0), (1, 1), (0, 1))
    y_peers = [device(flip_lo=l, flip_group=g) for l, g in y_flips]

    def remote(src, dst, send_sem, recv_sem, to):
        return pltpu.make_async_remote_copy(
            src_ref=src,
            dst_ref=dst,
            send_sem=send_sem,
            recv_sem=recv_sem,
            device_id=to,
            device_id_type=MESH,
        )

    pending = []

    def send(src, dst, send_sem, recv_sem, to):
        copy = remote(src, dst, send_sem, recv_sem, to)
        copy.start()
        pending.append(copy)

    def arrived(dst, recv_sem):
        remote(dst, dst, recv_sem, recv_sem, other_core).wait_recv()

    barrier = pltpu.get_barrier_semaphore()
    greeted = [right, left, other_core, *y_peers]
    greeted += [device(dz=d) for d in (STRIDE, -STRIDE, 1, -1, 2, -2)]
    greeted += [device(dz=d, flip_group=1) for d in (STRIDE, -STRIDE)]
    for peer in greeted:
        pl.semaphore_signal(barrier, inc=1, device_id=peer, device_id_type=MESH)

    olds = (old_master, old_moment, old_variance, old_grad)
    copies = [pltpu.make_async_copy(ref.at[0], flat_old.at[i], in_sems.at[i]) for i, ref in enumerate(olds)]
    copies.append(pltpu.make_async_copy(offsets_hbm, offsets, in_sems.at[4]))
    late = [
        pltpu.make_async_copy(tok_hbm, tok, in_sems.at[5]),
        pltpu.make_async_copy(cot_hbm, cot, in_sems.at[6]),
        pltpu.make_async_copy(counts_hbm, counts, in_sems.at[7]),
    ]
    for copy in copies + late:
        copy.start()

    for copy in copies:
        copy.wait()
    for r in range(window_rows):
        lanes = slice(r * LANES, (r + 1) * LANES)
        for i in range(4):
            old[i, r : r + 1, :] = flat_old[i, :, lanes]
    updated = adam_update(old[0], old[1], old[2], old[3], first_step)
    shape = (window_rows, LANES)
    position = (
        dp * (rows * LANES)
        - margin * LANES
        + lax.broadcasted_iota(jnp.int32, shape, 0) * LANES
        + lax.broadcasted_iota(jnp.int32, shape, 1)
    )
    slab = tensor * 2 + group
    low, high = offsets[slab, dp], offsets[slab, dp + 1]
    is_live = (position >= low) & (position < high)
    for i in range(3):
        live_state[i] = jnp.where(is_live, updated[i], F32(0.0))
    for i in range(3):
        edge_out[0, i] = live_state[i, rows + margin : window_rows, :]
        edge_out[1, i] = live_state[i, 0:margin, :]
    pl.semaphore_wait(barrier, len(greeted))
    send(edge_out.at[0], edge_in.at[0], edge_sems.at[0], edge_sems.at[2], right)
    send(edge_out.at[1], edge_in.at[1], edge_sems.at[1], edge_sems.at[3], left)
    for i in range(3):
        state[i] = live_state[i, margin : margin + rows, :]
    arrived(edge_in.at[0], edge_sems.at[2])
    arrived(edge_in.at[1], edge_sems.at[3])
    for i in range(3):
        state[i, 0:margin, :] += edge_in[0, i]
        state[i, rows - margin : rows, :] += edge_in[1, i]

    first = group == 0
    for i in range(3):
        top, bottom = state[i, 0:tile, :], state[i, tile:rows, :]
        tile_out[i] = jnp.where(first, bottom, top)
        kept[i] = jnp.where(first, top, bottom)

    line = w.at[group, y_lo, core]
    base = STRIDE * (half - 1) + 1

    def ring(k, direction):
        to = k - direction
        to = half if to == -half else to
        src, dst = base + STRIDE * k, base + STRIDE * to
        index = -k if direction > 0 else half + k
        send(line.at[src], line.at[dst], ring_send.at[index], z_recv.at[dst], device(dz=direction * STRIDE))

    def near(k):
        src = base + STRIDE * k
        for i, d in enumerate((-1, 1, -2)):
            send(line.at[src], line.at[src - d], near_send.at[i, k + half - 1], z_recv.at[src - d], device(dz=d))

    def along_y(k):
        block = k + half - 1
        for d in (-1, 1, 2):
            slot = base + STRIDE * k + d
            arrived(line.at[slot], z_recv.at[slot])
        piece = line.at[pl.ds(block * STRIDE, STRIDE)]
        for i, peer in enumerate(y_peers):
            send(piece, piece, y_send.at[i, block], y_recv.at[i, block], peer)

    def from_ring(k):
        slot = base + STRIDE * k
        arrived(line.at[slot], z_recv.at[slot])

    line[base] = state[0].astype(BF16)
    ring(0, 1)
    ring(0, -1)
    near(0)

    partner = y_peers[2]
    send(tile_out, tile_in, tile_sems.at[0], tile_sems.at[1], partner)

    for copy in late:
        copy.wait()
    low_slot = STRIDE * (half - 1) + 2
    group_z = 8
    group_rows = group_z * 2 * rows

    def transpose(i, carry):
        columns = tok[:, pl.ds(pl.multiple_of(i * group_rows, group_rows), group_rows)].T
        for n in range(group_z):
            nat = i * group_z + n
            lo = lax.div(nat, depth)
            slot = lax.rem(lax.rem(nat, depth) - z + low_slot + depth, depth)
            start = pl.multiple_of((lo * depth + slot) * (2 * rows), 2 * rows)
            tok_t[pl.ds(start, 2 * rows), :] = columns[n * 2 * rows : (n + 1) * 2 * rows, :]
        return carry

    steps = 2 * depth // group_z
    per_ring_step = steps // half
    lax.fori_loop(0, per_ring_step, transpose, 0)

    for k in range(1, half):
        from_ring(-k)
        ring(-k, 1)
        near(-k)
        from_ring(k)
        if k < half - 1:
            ring(k, -1)
        near(k)
        lax.fori_loop(k * per_ring_step, (k + 1) * per_ring_step, transpose, 0)
        along_y(1 - k)
        if k > 1:
            along_y(k - 1)
    from_ring(half)
    near(half)
    along_y(1 - half)
    along_y(half - 1)
    along_y(half)

    def to_core(i, lo, g):
        src = w.at[g, lo, core]
        send(src, src, core_send.at[i], core_recv.at[i], other_core)

    def lines(i):
        l, g = ((0, 0),) [0] if i == 0 else y_flips[i - 1]
        return (1 - y_lo if l else y_lo), (1 - group if g else group)

    to_core(0, y_lo, group)
    for i in range(3):
        lo, g = lines(i + 1)
        for block in range(members):
            src = w.at[g, lo, core, pl.ds(block * STRIDE, STRIDE)]
            arrived(src, y_recv.at[i, block])
        to_core(i + 1, lo, g)
    for i in range(4):
        lo, g = lines(i)
        arrived(w.at[g, lo, 1 - core], core_recv.at[i])

    def flatten(zz, carry):
        for lo in range(2):
            to_z = lax.rem(z + zz - base + depth, depth)
            start = pl.multiple_of((lo * depth + to_z) * (2 * rows), 2 * rows)
            for g in range(2):
                both = jnp.concatenate([w[g, lo, 0, zz], w[g, lo, 1, zz]], axis=0)
                w_flat[pl.ds(start, 2 * rows), g * LANES : (g + 1) * LANES] = both
        return carry

    lax.fori_loop(0, depth, flatten, 0)
    preact = jnp.dot(tok[...], w_flat[...], preferred_element_type=F32)
    sigmoid_z = jax.nn.sigmoid(preact)
    act[...] = (preact * sigmoid_z).astype(BF16)
    act_copy = pltpu.make_async_copy(act, act_out, act_sem)
    act_copy.start()
    derivative = sigmoid_z * (1.0 + preact * (1.0 - sigmoid_z))
    my_count = counts[dp * 2 + group]
    row_live = lax.broadcasted_iota(jnp.int32, preact.shape, 0) < my_count
    delta = jnp.where(row_live, cot[...].astype(F32) * derivative, F32(0.0)).astype(BF16)

    order = [half] + [s * k for k in range(half - 1, 0, -1) for s in (1, -1)] + [0]
    blocks = [k + half - 1 for k in order]
    for block in blocks:
        for lo in range(2):
            count = STRIDE * 2 * rows
            start = (lo * depth + block * STRIDE) * (2 * rows)
            part = jnp.dot(tok_t[pl.ds(start, count), :], delta, preferred_element_type=F32)
            for zz in range(STRIDE):
                for c in range(2):
                    top = (zz * 2 + c) * rows
                    for g in range(2):
                        parts[c, block, g, lo, zz] = part[top : top + rows, g * LANES : (g + 1) * LANES].astype(BF16)
        send(parts.at[1 - core, block], core_in.at[block], part_send.at[block], part_recv.at[block], other_core)
    def over_core(j):
        block = blocks[j]
        arrived(core_in.at[block], part_recv.at[block])
        both = parts[core, block].astype(F32) + core_in[block].astype(F32)
        parts[core, block] = both.astype(BF16)
        for i, (l, g) in enumerate(y_flips):
            lo = 1 - y_lo if l else y_lo
            gg = 1 - group if g else group
            send(parts.at[core, block, gg, lo], y_in.at[i, block], sum_send.at[i, block], sum_recv.at[i, block], y_peers[i])

    def over_y(j):
        block = blocks[j]
        total = parts[core, block, group, y_lo].astype(F32)
        for i in range(3):
            arrived(y_in.at[i, block], sum_recv.at[i, block])
            total += y_in[i, block].astype(F32)
        z_sum[block] = total.astype(BF16)
        for i, dz in enumerate((-2, -1, 1)):
            src = z_sum.at[block, 2 + dz]
            send(src, near_in.at[i, block], window_send.at[i, block], window_recv.at[i, block], device(dz=dz))

    def halves(i, total, dz):
        ends[i, 0] = total[0:tile]
        ends[i, 1] = total[tile:rows]
        ends_out[i] = ends[i].astype(BF16)
        for own, to in ((1, device(dz=dz)), (0, device(dz=dz, flip_group=1))):
            if own and dz == 0:
                continue
            half_rows = group if own else 1 - group
            n = 4 if dz == 0 else 2 * i + 1 - own
            send(ends_out.at[i, half_rows], ends_in.at[n], end_sems.at[0, n], end_sems.at[1, n], to)

    def over_ring(j):
        block, k = blocks[j], order[j]
        total = z_sum[block, 2].astype(F32)
        for i in range(3):
            arrived(near_in.at[i, block], window_recv.at[i, block])
            total += near_in[i, block].astype(F32)
        if k == 0:
            halves(2, total, 0)
            own_sum = jnp.where(first, total[0:tile], total[tile:rows])
            for n in range(5):
                arrived(ends_in.at[n], end_sems.at[1, n])
            mine = own_sum + ends_in[0].astype(F32) + ends_in[2].astype(F32)
            theirs = ends_in[1].astype(F32) + ends_in[3].astype(F32) + ends_in[4].astype(F32)
            return mine, theirs
        if k >= 0 and k < half:
            s = half - 1 - k
            arrived(plus_in.at[s], plus_sems.at[1, s])
            total += plus_in[s].astype(F32)
        if k <= 0 and -k < half - 1:
            s = half - 2 + k
            arrived(minus_in.at[s], minus_sems.at[1, s])
            total += minus_in[s].astype(F32)
        if k == 1 or k == -1:
            halves(0 if k > 0 else 1, total, STRIDE * k)
        elif k > 0:
            s = half - k
            plus_out[s] = total.astype(BF16)
            send(plus_out.at[s], plus_in.at[s], plus_sems.at[0, s], plus_sems.at[1, s], device(dz=STRIDE))
        elif k < 0:
            s = half - 1 + k
            minus_out[s] = total.astype(BF16)
            send(minus_out.at[s], minus_in.at[s], minus_sems.at[0, s], minus_sems.at[1, s], device(dz=-STRIDE))
        return total

    for j in range(IN_FLIGHT):
        over_core(j)
    for j in range(members + 1):
        if j < members:
            over_y(j)
        if j + IN_FLIGHT < members:
            over_core(j + IN_FLIGHT)
        if j >= 1:
            gradient = over_ring(j - 1)

    arrived(tile_in, tile_sems.at[1])
    for lanes, old_state, summed in ((group, kept, gradient[0]), (1 - group, tile_in, gradient[1])):
        new = adam_update(old_state[0], old_state[1], old_state[2], summed, second_step)
        start = pl.multiple_of(lanes * LANES, LANES)
        for i in range(3):
            state_out[i, :, pl.ds(start, LANES)] = new[i]
    act_copy.wait()
    for copy in pending:
        copy.wait_send()


def finish(act, state, act_out, master_out, moment_out, variance_out):
    act_out[...] = act[...]
    for i, ref in enumerate((master_out, moment_out, variance_out)):
        ref[...] = state[i]


def solution(mesh):
    dp_size = mesh.shape["dp"]
    depth = dp_size // 4
    members = depth // STRIDE
    half = members // 2

    def local(tokens, cotangent, counts, old_offsets, old_master, old_moment, old_variance, old_grad):
        token_rows, width = tokens.shape
        window_rows = old_master.shape[-1] // LANES
        rows = width // dp_size
        margin = (window_rows - rows) // 2
        tile = rows // 2
        out = jax.ShapeDtypeStruct((tile, 2 * LANES), F32)
        piece = (rows, LANES)
        vmem = pl.BlockSpec(memory_space=pltpu.VMEM)
        dma = pltpu.SemaphoreType.DMA
        act_shape = jax.ShapeDtypeStruct(cotangent.shape, BF16)
        act, new_state = pl.pallas_call(
            functools.partial(kernel, dp_size),
            out_shape=(act_shape, jax.ShapeDtypeStruct((3, tile, 2 * LANES), F32)),
            in_specs=[pl.BlockSpec(memory_space=pltpu.HBM)] * 8,
            out_specs=(pl.BlockSpec(memory_space=pltpu.HBM), vmem),
            scratch_shapes=[
                pltpu.SMEM(old_offsets.shape, jnp.int32),
                pltpu.SMEM(counts.shape, jnp.int32),
                pltpu.VMEM(cotangent.shape, BF16),
                pltpu.VMEM((4, 1, old_master.shape[-1]), F32),
                pltpu.VMEM((token_rows, width), BF16),
                pltpu.VMEM((width, token_rows), BF16),
                pltpu.VMEM((4, window_rows, LANES), F32),
                pltpu.VMEM((3, window_rows, LANES), F32),
                pltpu.VMEM((2, 3, margin, LANES), F32),
                pltpu.VMEM((2, 3, margin, LANES), F32),
                pltpu.VMEM((3, *piece), F32),
                pltpu.VMEM((2, 2, 2, depth, *piece), BF16),
                pltpu.VMEM((width, 2 * LANES), BF16),
                pltpu.VMEM((2, members, 2, 2, STRIDE, *piece), BF16),
                pltpu.VMEM((members, 2, 2, STRIDE, *piece), BF16),
                pltpu.VMEM((3, members, STRIDE, *piece), BF16),
                pltpu.VMEM((members, STRIDE, *piece), BF16),
                pltpu.VMEM((3, members, *piece), BF16),
                pltpu.VMEM((half, *piece), BF16),
                pltpu.VMEM((half, *piece), BF16),
                pltpu.VMEM((half, *piece), BF16),
                pltpu.VMEM((half, *piece), BF16),
                pltpu.VMEM((3, tile, LANES), F32),
                pltpu.VMEM((3, tile, LANES), F32),
                pltpu.VMEM((3, tile, LANES), F32),
                pltpu.VMEM((3, 2, tile, LANES), F32),
                pltpu.VMEM((3, 2, tile, LANES), BF16),
                pltpu.VMEM((5, tile, LANES), BF16),
                pltpu.VMEM(cotangent.shape, BF16),
                dma((8,)),
                dma((4,)),
                dma((2 * half,)),
                dma((depth,)),
                dma((3, members)),
                dma((3, members)),
                dma((3, members)),
                dma((4,)),
                dma((4,)),
                dma((members,)),
                dma((members,)),
                dma((3, members)),
                dma((3, members)),
                dma((3, members)),
                dma((3, members)),
                dma((2, half)),
                dma((2, half)),
                dma((2,)),
                dma((2, 5)),
                dma(()),
            ],
            compiler_params=pltpu.CompilerParams(
                collective_id=0, has_side_effects=True, vmem_limit_bytes=60 * 1024 * 1024
            ),
        )(old_offsets, counts, tokens, cotangent, old_master, old_moment, old_variance, old_grad)
        return pl.pallas_call(
            finish,
            out_shape=(act_shape, out, out, out),
            in_specs=[vmem] * 2,
            out_specs=(vmem,) * 4,
        )(act, new_state)

    state_spec = P(("tensor", "group"), "dp", None)
    row_spec = P(("dp", "group"), "tensor")
    return jax.shard_map(
        local,
        mesh=mesh,
        in_specs=(P(("dp", "group"), None), row_spec, P(), P(), state_spec, state_spec, state_spec, state_spec),
        out_specs=(row_spec,) * 4,
        check_vma=False,
    )
```
